256 devices in a mesh: row: 32 (over y, z_lo, core), col: 8 (over x, z_hi).
Axes of the slice: x: 4, y: 4, z: 8 (z_hi: 2, z_lo: 4; z = z_hi * 4 + z_lo), core: 2. Of those that a mesh axis runs over, the one named last changes fastest.
Arguments:
- features: bfloat16 [32768, 512], P(('row', 'col')), may hold values from -6 to 6
- edge_tiles: bfloat16 [8192, 128, 128], P(('row', 'col')), may hold values from 0 to 1
- tile_rows: int32 [256, 32], P(('row', 'col')), may hold values from 0 to 7
- tile_cols: int32 [256, 32], P(('row', 'col')), may hold values from 0 to 31
- tile_count: int32 [256], P(('row', 'col')), may hold values from 8 to 32, as said below
- node_order: int32 [256, 128], P(('row', 'col')), may hold values from 0 to 127, each once within a row
- w_self: bfloat16 [512, 512], replicated, may hold values from -0.25 to 0.25
- w_neigh: bfloat16 [512, 512], replicated, may hold values from -12 to 12
- bias_term: bfloat16 [512], replicated, may hold values from -3 to 3
- cotangent: bfloat16 [32768, 512], P(('row', 'col')), may hold values from -6 to 6
Outputs:
- activations: bfloat16 [32768, 512], P(('row', 'col'))
- feature_grad: float32 [32768, 512], P(('row', 'col'))
- self_grad: float32 [512, 512], replicated
- neigh_grad: float32 [512, 512], replicated
- bias_grad: float32 [512], replicated
The draws below stay inside these ranges and needn't reach their ends.
Inputs may be any that keep to these rules, and one draw needn't show every extreme that they name: Only the first tile_count[b] slots of block b's tile list are valid; later slots are padding and are ignored. The busiest block holds 32 tiles and the lightest 32 // 4. `tile_rows`: tile coordinates may repeat within a block's list. `tile_cols`: tile coordinates may repeat within a block's list.
All inputs are finite; a program needn't handle non-finite values.
Results may differ from the reference program's by a relative error of at most 0.0042.
Values may be sent and summed in bfloat16 or wider, within the bound.
A program may use at most 64 MiB of HBM per device.

```python
import jax
import jax.numpy as jnp
from jax import lax

FEAT = 512
TILE = 128
NODE_DEV = 128
TMAX = 32
NODES = 32768
ROW_TILES = 8
COL_TILES = 32
N_ROW = 32
N_COL = 8


def draw_tile_count(key, part):
    block_total = NODES // NODE_DEV
    first_key, second_key = jax.random.split(key)
    spread_draw = jax.random.randint(first_key, (block_total,), 0, 64)
    lowest = TMAX // 4
    counts = lowest + (TMAX - lowest) * spread_draw * spread_draw // 3969
    picks = jax.random.permutation(second_key, block_total)
    counts = counts.at[picks[0]].set(TMAX).at[picks[1]].set(lowest)
    return counts.astype(jnp.int32)


def place_ends(entries, rng, low, largest):
    longest = entries.shape.index(max(entries.shape))
    spots = []
    for shift in (0, 1):
        where = [jax.random.randint(jax.random.fold_in(rng, axis), (), 0, length) for axis, length in enumerate(entries.shape)]
        where[longest] = (where[longest] + shift) % entries.shape[longest]
        spots.append(tuple(where))
    return entries.at[spots[0]].set(low).at[spots[1]].set(largest)


def levels(own_key, shape, cuts, least, high):
    factor_of = 1.0
    for axis_at, parts in cuts:
        heights = jax.random.uniform(jax.random.fold_in(jax.random.fold_in(own_key, 6), axis_at), (parts,), jnp.float32, least / len(cuts), high / len(cuts))
        factor_of = factor_of * jnp.repeat(jnp.exp(heights), shape[axis_at] // parts).reshape((-1,) + (1,) * (len(shape) - 1 - axis_at))
    return factor_of


def gaussian(rng, extent, width, most, cuts=(), kind=jnp.bfloat16):
    entries = jax.random.normal(rng, extent, jnp.float32) * width
    if len(cuts) > 0:
        entries = levels(rng, extent, cuts, -0.22, 0.18) * entries
    return jnp.clip(entries, min=-most, max=most).astype(kind)


def setup_inputs(seed: int = 0) -> dict:
    streams_of = jax.random.split(jax.random.key(seed), 11)
    features = gaussian(streams_of[0], (NODES, FEAT), 1.0, 6.0, ((0, 256),))
    edge_tiles = jnp.clip(1.0 * jax.random.uniform(streams_of[1], (NODES // NODE_DEV * TMAX, TILE, TILE), jnp.float32) ** levels(streams_of[1], (NODES // NODE_DEV * TMAX, TILE, TILE), ((0, 256),), -0.2, 0.2), 0.0, 1.0).astype(jnp.bfloat16)
    tile_rows = place_ends(jax.random.randint(streams_of[2], (NODES // NODE_DEV, TMAX), 0, ROW_TILES), jax.random.fold_in(streams_of[2], 1), 0, ROW_TILES - 1).astype(jnp.int32)
    tile_cols = place_ends(jax.random.randint(streams_of[3], (NODES // NODE_DEV, TMAX), 0, COL_TILES), jax.random.fold_in(streams_of[3], 1), 0, COL_TILES - 1).astype(jnp.int32)
    tile_count = draw_tile_count(jax.random.fold_in(streams_of[10], 71), 0)
    node_order = jax.vmap(lambda own: jax.random.permutation(own, NODE_DEV))(jax.random.split(streams_of[5], (NODES // NODE_DEV))).reshape((NODES // NODE_DEV, NODE_DEV)).astype(jnp.int32)
    w_self = gaussian(streams_of[6], (FEAT, FEAT), FEAT ** -0.5, 0.25)
    w_neigh = gaussian(streams_of[7], (FEAT, FEAT), 2.0, 12.0)
    bias_term = gaussian(streams_of[8], (FEAT,), 0.5, 3.0)
    cotangent = gaussian(streams_of[9], (NODES, FEAT), 1.0, 6.0, ((0, 256),))
    return {"features": features, "edge_tiles": edge_tiles, "tile_rows": tile_rows, "tile_cols": tile_cols, "tile_count": tile_count, "node_order": node_order, "w_self": w_self, "w_neigh": w_neigh, "bias_term": bias_term, "cotangent": cotangent}


def reference(features, edge_tiles, tile_rows, tile_cols, tile_count, node_order, w_self, w_neigh, bias_term, cotangent):
    blocks = N_ROW * N_COL
    stored = features.reshape(blocks, NODE_DEV, FEAT)
    ordered = jnp.take_along_axis(stored, node_order[:, :, None], axis=1)
    flat_rows = ordered.reshape(NODES, FEAT)
    column_sets = ordered.reshape(N_ROW, N_COL, NODE_DEV, FEAT).transpose(1, 0, 2, 3).reshape(N_COL, COL_TILES, TILE, FEAT)
    tile_sets = edge_tiles.reshape(blocks, TMAX, TILE, TILE)
    slots = jnp.arange(TMAX, dtype=jnp.int32)
    block_ids = jnp.arange(blocks, dtype=jnp.int32)

    def forward_step(carry, block_id):
        summed, degree = carry
        row_id = block_id // N_COL
        col_id = block_id % N_COL
        weights = tile_sets[block_id].astype(jnp.float32)
        live_mask = (slots < tile_count[block_id]).astype(jnp.float32)
        picked = column_sets[col_id][tile_cols[block_id]].astype(jnp.float32)
        products = jnp.einsum("tij,tjf->tif", weights, picked) * live_mask[:, None, None]
        row_terms = jax.ops.segment_sum(products, tile_rows[block_id], num_segments=ROW_TILES)
        row_degree = jax.ops.segment_sum(jnp.sum(weights, axis=2) * live_mask[:, None], tile_rows[block_id], num_segments=ROW_TILES)
        return (summed.at[row_id].add(row_terms), degree.at[row_id].add(row_degree)), None

    start_sums = (jnp.zeros((N_ROW, ROW_TILES, TILE, FEAT), jnp.float32), jnp.zeros((N_ROW, ROW_TILES, TILE), jnp.float32))
    (summed, degree), _ = lax.scan(forward_step, start_sums, block_ids)
    summed = summed.reshape(NODES, FEAT)
    degree = degree.reshape(NODES)
    inverse_degree = 1.0 / (1.0 + degree)
    neigh_mean = (summed * inverse_degree[:, None]).astype(jnp.bfloat16)
    preact = (jnp.dot(flat_rows, w_self, preferred_element_type=jnp.float32)
              + jnp.dot(neigh_mean, w_neigh, preferred_element_type=jnp.float32)
              + bias_term.astype(jnp.float32))
    activations = (jnp.maximum(preact, 0.0) + jnp.expm1(jnp.minimum(preact, 0.0))).astype(jnp.bfloat16)
    grad_pre = (cotangent.astype(jnp.float32) * jnp.exp(jnp.minimum(preact, 0.0))).astype(jnp.bfloat16)
    self_grad = jnp.dot(flat_rows.T, grad_pre, preferred_element_type=jnp.float32)
    neigh_grad = jnp.dot(neigh_mean.T, grad_pre, preferred_element_type=jnp.float32)
    bias_grad = jnp.sum(grad_pre.astype(jnp.float32), axis=0)
    agg_grad = (jnp.dot(grad_pre, w_neigh.T, preferred_element_type=jnp.float32) * inverse_degree[:, None]).astype(jnp.bfloat16)
    row_sets = agg_grad.reshape(N_ROW, ROW_TILES, TILE, FEAT)

    def backward_step(carry, block_id):
        row_id = block_id // N_COL
        col_id = block_id % N_COL
        weights = tile_sets[block_id].astype(jnp.float32)
        live_mask = (slots < tile_count[block_id]).astype(jnp.float32)
        picked = row_sets[row_id][tile_rows[block_id]].astype(jnp.float32)
        products = jnp.einsum("tij,tif->tjf", weights, picked) * live_mask[:, None, None]
        col_terms = jax.ops.segment_sum(products, tile_cols[block_id], num_segments=COL_TILES)
        return carry.at[col_id].add(col_terms), None

    column_grads, _ = lax.scan(backward_step, jnp.zeros((N_COL, COL_TILES, TILE, FEAT), jnp.float32), block_ids)
    spread = column_grads.reshape(N_COL, N_ROW, NODE_DEV, FEAT).transpose(1, 0, 2, 3).reshape(NODES, FEAT)
    local_grad = jnp.dot(grad_pre, w_self.T, preferred_element_type=jnp.float32) + spread
    inverse_order = jnp.argsort(node_order, axis=1).astype(jnp.int32)
    feature_grad = jnp.take_along_axis(local_grad.reshape(blocks, NODE_DEV, FEAT), inverse_order[:, :, None], axis=1).reshape(NODES, FEAT)
    return (activations, feature_grad, self_grad, neigh_grad, bias_grad)
```

```python
import functools

import jax
import jax.numpy as jnp
from jax import lax
from jax.experimental import pallas as pl
from jax.experimental.pallas import tpu as pltpu
from jax.sharding import PartitionSpec as P

LINE = 4
CORES = 2
HALVES = 2
ROWS = LINE * LINE * CORES
COLS = LINE * HALVES
F32 = jnp.float32
BF16 = jnp.bfloat16


def row_place():
    me = lax.axis_index("row")
    return me // (LINE * CORES), (me // CORES) % LINE, me % CORES


def row_of(y, z, core):
    return (y * LINE + z) * CORES + core


def z_partners(z):
    return (z + 1 - 2 * (z % 2), (z + 2) % LINE, LINE - 1 - z)


def greet(targets):
    barrier = pltpu.get_barrier_semaphore()
    for target in targets:
        pl.semaphore_signal(barrier, inc=1, device_id=target, device_id_type=pl.DeviceIdType.MESH)
    pl.semaphore_wait(barrier, len(targets))


def start_copy(source, target, send_sem, recv_sem, device):
    copy = pltpu.make_async_remote_copy(
        src_ref=source,
        dst_ref=target,
        send_sem=send_sem,
        recv_sem=recv_sem,
        device_id=device,
        device_id_type=pl.DeviceIdType.MESH,
    )
    copy.start()
    return copy


def arrived(target, recv_sem):
    pltpu.make_async_copy(target, target, recv_sem).wait()


def one_hot_order(order_ref, size):
    return order_ref[...] == lax.broadcasted_iota(jnp.int32, (size, size), 0)


def gather_kernel(order_ref, feat_ref, column_ref, send_sem, recv_sem, half_sem):
    y, z, core = row_place()
    size = feat_ref.shape[0]
    half = size // 2
    up, down, far = (y + 1) % LINE, (y + LINE - 1) % LINE, (y + 2) % LINE
    along = z_partners(z)
    other = {"row": row_of(y, z, 1 - core)}
    to_up = {"row": row_of(up, z, core)}
    to_down = {"row": row_of(down, z, core)}
    to_along = [{"row": row_of(y, place, core)} for place in along]
    me = row_of(y, z, core)
    chosen = one_hot_order(order_ref, size).astype(F32).astype(BF16)
    column_ref[me] = lax.dot_general(
        chosen, feat_ref[...], (((0,), (0,)), ((), ())), preferred_element_type=F32
    ).astype(BF16)
    greet([other, to_up, to_down, *to_along])
    sent = []

    def push(block, device):
        sent.append(
            start_copy(
                column_ref.at[block], column_ref.at[block], send_sem.at[len(sent)], recv_sem.at[block], device
            )
        )

    def push_half(block, slot, part, device):
        rows = pl.ds(part * half, half)
        sent.append(
            start_copy(
                column_ref.at[block, rows],
                column_ref.at[block, rows],
                send_sem.at[len(sent)],
                half_sem.at[slot, part],
                device,
            )
        )

    def wait_block(block):
        arrived(column_ref.at[block], recv_sem.at[block])

    def from_line(index):
        block = row_of(y, along[index], core)
        wait_block(block)
        push(block, to_up)
        push(block, to_down)
        push(block, other)

    places = (z, *along)

    def from_ring(index):
        below, above = row_of(down, places[index], core), row_of(up, places[index], core)
        wait_block(below)
        push_half(below, index, 0, to_up)
        push(below, other)
        wait_block(above)
        push_half(above, index, 1, to_down)
        push(above, other)

    def from_far(index):
        block = row_of(far, places[index], core)
        for part in range(2):
            arrived(column_ref.at[block, pl.ds(part * half, half)], half_sem.at[index, part])
        push(block, other)

    push(me, to_up)
    push(me, to_down)
    for device in to_along:
        push(me, device)
    push(me, other)
    from_line(0)
    from_ring(0)
    from_line(1)
    from_ring(1)
    from_line(2)
    from_far(0)
    from_ring(2)
    from_far(1)
    from_ring(3)
    from_far(2)
    from_far(3)
    for place in range(LINE * LINE):
        wait_block(place * CORES + 1 - core)
    for copy in sent:
        copy.wait_send()


def gather_rows(order, features):
    size, channels = features.shape
    return pl.pallas_call(
        gather_kernel,
        out_shape=jax.ShapeDtypeStruct((ROWS, size, channels), BF16),
        in_specs=[pl.BlockSpec(memory_space=pltpu.VMEM)] * 2,
        out_specs=pl.BlockSpec(memory_space=pltpu.VMEM),
        scratch_shapes=[
            pltpu.SemaphoreType.DMA((35,)),
            pltpu.SemaphoreType.DMA((ROWS,)),
            pltpu.SemaphoreType.DMA((LINE, 2)),
        ],
        compiler_params=pltpu.CompilerParams(collective_id=0, has_side_effects=True),
        name="gather_rows",
    )(order, features)


def forward_kernel(count_ref, rows_ref, cols_ref, tiles_ref, column_ref, sums_ref, degree_ref):
    size = tiles_ref.shape[1]
    sums_ref[...] = jnp.zeros_like(sums_ref)
    degree_ref[...] = jnp.zeros_like(degree_ref)
    ones = jnp.ones((8, size), BF16)

    def advance(slot, carry):
        at = rows_ref[0, slot]
        tile = tiles_ref[slot]
        sums_ref[at] += jnp.dot(tile, column_ref[cols_ref[0, slot]], preferred_element_type=F32)
        degree_ref[at] += lax.dot_general(
            ones, tile, (((1,), (1,)), ((), ())), preferred_element_type=F32
        )
        return carry

    lax.fori_loop(0, count_ref[0], advance, 0)


def forward_sums(count, rows_at, cols_at, tiles, column):
    _, size, channels = column.shape
    return pl.pallas_call(
        forward_kernel,
        out_shape=(
            jax.ShapeDtypeStruct((COLS, size, channels), F32),
            jax.ShapeDtypeStruct((COLS, 8, size), F32),
        ),
        in_specs=[pl.BlockSpec(memory_space=pltpu.SMEM)] * 3 + [pl.BlockSpec(memory_space=pltpu.VMEM)] * 2,
        out_specs=(pl.BlockSpec(memory_space=pltpu.VMEM),) * 2,
        name="forward_sums",
    )(count, rows_at, cols_at, tiles, column)


def middle_kernel(
    sums_ref,
    degree_ref,
    own_ref,
    w_self_ref,
    w_neigh_ref,
    bias_ref,
    cot_ref,
    act_ref,
    grad_ref,
    self_ref,
    neigh_ref,
    bias_grad_ref,
    agg_ref,
    far_out,
    near_out,
    mixed_out,
    cross_out,
    far_in,
    near_in,
    mixed_in,
    cross_in,
    degree_in,
    send_sem,
    far_sem,
    near_sem,
    mixed_sem,
    cross_sem,
    degree_sem,
    agg_sem,
    agg_half_sem,
):
    here = lax.axis_index("col")
    x, side = here // HALVES, here % HALVES
    size = own_ref.shape[0]
    half = size // 2
    low, high = pl.ds(0, half), pl.ds(half, half)
    up, down, far = (x + 1) % LINE, (x + LINE - 1) % LINE, (x + 2) % LINE
    sides = (1 - side, side)

    def col_of(place, where):
        return place * HALVES + where

    to_up = {"col": col_of(up, side)}
    to_down = {"col": col_of(down, side)}
    to_cross = {"col": col_of(x, 1 - side)}
    peers = [to_up, to_down, to_cross, {"col": col_of(far, side)}]
    peers += [{"col": col_of(place, 1 - side)} for place in (up, down, far)]
    sent = []

    def push(source, target, recv_sem, device):
        sent.append(start_copy(source, target, send_sem.at[len(sent)], recv_sem, device))

    greet(peers)
    for offset in range(1, COLS):
        owner = (here + offset) % COLS
        push(degree_ref.at[owner], degree_in.at[offset], degree_sem.at[offset], {"col": owner})
    for phase in range(2):
        block = col_of(far, sides[phase])
        far_out[phase] = sums_ref[block].astype(BF16)
        push(far_out.at[phase, low], far_in.at[phase, 0], far_sem.at[phase, 0], to_up)
        push(far_out.at[phase, high], far_in.at[phase, 1], far_sem.at[phase, 1], to_down)
        near_out[phase, 0] = sums_ref[col_of(up, sides[phase]), high].astype(BF16)
        near_out[phase, 1] = sums_ref[col_of(down, sides[phase]), low].astype(BF16)
        push(near_out.at[phase, 0], near_in.at[phase, 0], near_sem.at[phase, 0], to_up)
        push(near_out.at[phase, 1], near_in.at[phase, 1], near_sem.at[phase, 1], to_down)
    own = own_ref[...]
    self_term = jnp.dot(own, w_self_ref[...], preferred_element_type=F32) + bias_ref[...].astype(F32)

    def gathered(phase):
        arrived(far_in.at[phase, 0], far_sem.at[phase, 0])
        mixed_out[phase, 0] = (
            sums_ref[col_of(up, sides[phase]), low] + far_in[phase, 0].astype(F32)
        ).astype(BF16)
        push(mixed_out.at[phase, 0], mixed_in.at[phase, 0], mixed_sem.at[phase, 0], to_up)
        arrived(far_in.at[phase, 1], far_sem.at[phase, 1])
        mixed_out[phase, 1] = (
            sums_ref[col_of(down, sides[phase]), high] + far_in[phase, 1].astype(F32)
        ).astype(BF16)
        push(mixed_out.at[phase, 1], mixed_in.at[phase, 1], mixed_sem.at[phase, 1], to_down)
        for part in range(2):
            arrived(near_in.at[phase, part], near_sem.at[phase, part])
        for part in range(2):
            arrived(mixed_in.at[phase, part], mixed_sem.at[phase, part])
        mine = sums_ref[col_of(x, sides[phase])]
        upper = mine[:half] + mixed_in[phase, 0].astype(F32) + near_in[phase, 1].astype(F32)
        lower = mine[half:] + near_in[phase, 0].astype(F32) + mixed_in[phase, 1].astype(F32)
        return jnp.concatenate([upper, lower], axis=0)

    cross_out[...] = gathered(0).astype(BF16)
    push(cross_out, cross_in, cross_sem.at[0], to_cross)
    own_sum = gathered(1)
    degree = degree_ref[here]
    for offset in range(1, COLS):
        arrived(degree_in.at[offset], degree_sem.at[offset])
        degree += degree_in[offset]
    inverse = jnp.broadcast_to((1.0 / (1.0 + degree))[:1], (size, size)).T
    inverse = jnp.concatenate([inverse] * (own.shape[1] // size), axis=1)
    arrived(cross_in, cross_sem.at[0])
    own_sum += cross_in[...].astype(F32)
    neigh_mean = (own_sum * inverse).astype(BF16)
    preact = self_term + jnp.dot(neigh_mean, w_neigh_ref[...], preferred_element_type=F32)
    below = jnp.minimum(preact, 0.0)
    slope = cot_ref[...].astype(F32) * jnp.exp(below)
    grad_pre = slope.astype(BF16)
    agg_ref[here] = (
        lax.dot_general(grad_pre, w_neigh_ref[...], (((1,), (1,)), ((), ())), preferred_element_type=F32)
        * inverse
    ).astype(BF16)
    push(agg_ref.at[here], agg_ref.at[here], agg_sem.at[here], to_cross)
    push(agg_ref.at[here], agg_ref.at[here], agg_sem.at[here], to_up)
    push(agg_ref.at[here], agg_ref.at[here], agg_sem.at[here], to_down)
    grad_ref[...] = grad_pre
    bent = jnp.tanh(0.5 * below)
    act_ref[...] = (jnp.maximum(preact, 0.0) + 2.0 * bent / (1.0 - bent)).astype(BF16)

    def round_ring(where, slot):
        from_down, from_up = col_of(down, where), col_of(up, where)
        arrived(agg_ref.at[from_down], agg_sem.at[from_down])
        push(agg_ref.at[from_down, low], agg_ref.at[from_down, low], agg_half_sem.at[slot, 0], to_up)
        arrived(agg_ref.at[from_up], agg_sem.at[from_up])
        push(agg_ref.at[from_up, high], agg_ref.at[from_up, high], agg_half_sem.at[slot, 1], to_down)

    round_ring(side, 0)
    self_ref[...] = lax.dot_general(own, grad_pre, (((0,), (0,)), ((), ())), preferred_element_type=F32)
    cross = col_of(x, 1 - side)
    arrived(agg_ref.at[cross], agg_sem.at[cross])
    push(agg_ref.at[cross], agg_ref.at[cross], agg_sem.at[cross], to_up)
    push(agg_ref.at[cross], agg_ref.at[cross], agg_sem.at[cross], to_down)
    neigh_ref[...] = lax.dot_general(
        neigh_mean, grad_pre, (((0,), (0,)), ((), ())), preferred_element_type=F32
    )
    bias_grad_ref[...] = jnp.sum(grad_pre.astype(F32), axis=0, keepdims=True)
    round_ring(1 - side, 1)
    for slot, where in enumerate((side, 1 - side)):
        block = col_of(far, where)
        arrived(agg_ref.at[block, low], agg_half_sem.at[slot, 0])
        arrived(agg_ref.at[block, high], agg_half_sem.at[slot, 1])
    for copy in sent:
        copy.wait_send()


def middle(sums, degree, own, w_self, w_neigh, bias, cotangent):
    size, channels = own.shape
    half = size // 2
    wide = w_self.shape[0]
    halves = functools.partial(pltpu.VMEM, dtype=BF16)
    return pl.pallas_call(
        middle_kernel,
        out_shape=(
            jax.ShapeDtypeStruct((size, channels), BF16),
            jax.ShapeDtypeStruct((size, channels), BF16),
            jax.ShapeDtypeStruct((wide, wide), F32),
            jax.ShapeDtypeStruct((wide, wide), F32),
            jax.ShapeDtypeStruct((1, wide), F32),
            jax.ShapeDtypeStruct((COLS, size, channels), BF16),
        ),
        in_specs=[pl.BlockSpec(memory_space=pltpu.VMEM)] * 7,
        out_specs=(pl.BlockSpec(memory_space=pltpu.VMEM),) * 6,
        scratch_shapes=[
            halves((2, size, channels)),
            halves((2, 2, half, channels)),
            halves((2, 2, half, channels)),
            halves((size, channels)),
            halves((2, 2, half, channels)),
            halves((2, 2, half, channels)),
            halves((2, 2, half, channels)),
            halves((size, channels)),
            pltpu.VMEM((COLS, 8, size), F32),
            pltpu.SemaphoreType.DMA((30,)),
            pltpu.SemaphoreType.DMA((2, 2)),
            pltpu.SemaphoreType.DMA((2, 2)),
            pltpu.SemaphoreType.DMA((2, 2)),
            pltpu.SemaphoreType.DMA((1,)),
            pltpu.SemaphoreType.DMA((COLS,)),
            pltpu.SemaphoreType.DMA((COLS,)),
            pltpu.SemaphoreType.DMA((2, 2)),
        ],
        compiler_params=pltpu.CompilerParams(collective_id=1, has_side_effects=True),
        name="middle",
    )(sums, degree, own, w_self, w_neigh, bias, cotangent)


def backward_kernel(count_ref, rows_ref, cols_ref, tiles_ref, agg_ref, terms_ref, total):
    total[...] = jnp.zeros_like(total)

    def advance(slot, carry):
        at = cols_ref[0, slot]
        total[at] += lax.dot_general(
            tiles_ref[slot],
            agg_ref[rows_ref[0, slot]],
            (((0,), (0,)), ((), ())),
            preferred_element_type=F32,
        )
        return carry

    lax.fori_loop(0, count_ref[0], advance, 0)

    def put(block, carry):
        terms_ref[block % CORES, block // CORES] = total[block].astype(BF16)
        return carry

    lax.fori_loop(0, ROWS, put, 0)


def backward_terms(count, rows_at, cols_at, tiles, agg):
    _, size, channels = agg.shape
    return pl.pallas_call(
        backward_kernel,
        out_shape=jax.ShapeDtypeStruct((CORES, ROWS // CORES, size, channels), BF16),
        in_specs=[pl.BlockSpec(memory_space=pltpu.SMEM)] * 3 + [pl.BlockSpec(memory_space=pltpu.VMEM)] * 2,
        out_specs=pl.BlockSpec(memory_space=pltpu.VMEM),
        scratch_shapes=[pltpu.VMEM((ROWS, size, channels), F32)],
        name="backward_terms",
    )(count, rows_at, cols_at, tiles, agg)


def scatter_kernel(
    terms_ref,
    grad_ref,
    w_self_ref,
    order_ref,
    out_ref,
    pair_in,
    far_out,
    near_out,
    mixed_out,
    line_out,
    far_in,
    near_in,
    mixed_in,
    line_in,
    send_sem,
    pair_sem,
    far_sem,
    near_sem,
    mixed_sem,
    line_sem,
):
    y, z, core = row_place()
    size = grad_ref.shape[0]
    half = size // 2
    low, high = pl.ds(0, half), pl.ds(half, half)
    up, down, far = (y + 1) % LINE, (y + LINE - 1) % LINE, (y + 2) % LINE
    along = z_partners(z)
    places = (along[2], along[1], along[0], z)
    other = {"row": row_of(y, z, 1 - core)}
    to_up = {"row": row_of(up, z, core)}
    to_down = {"row": row_of(down, z, core)}
    to_along = [{"row": row_of(y, place, core)} for place in along]
    sent = []

    def push(source, target, recv_sem, device):
        sent.append(start_copy(source, target, send_sem.at[len(sent)], recv_sem, device))

    greet([other, to_up, to_down, *to_along])
    for ring in (far, up, down, y):
        for place in places:
            block = ring * LINE + place
            push(terms_ref.at[1 - core, block], pair_in.at[block], pair_sem.at[block], other)

    def paired(ring, place, rows):
        block = ring * LINE + place
        return terms_ref[core, block, rows].astype(F32) + pair_in[block, rows].astype(F32)

    def wait_pair(ring, place):
        block = ring * LINE + place
        arrived(pair_in.at[block], pair_sem.at[block])

    everything = pl.ds(0, size)
    for index, place in enumerate(places):
        wait_pair(far, place)
        far_out[index] = paired(far, place, everything).astype(BF16)
        push(far_out.at[index, low], far_in.at[index, 0], far_sem.at[index, 0], to_up)
        push(far_out.at[index, high], far_in.at[index, 1], far_sem.at[index, 1], to_down)
    for index, place in enumerate(places):
        wait_pair(up, place)
        near_out[index, 0] = paired(up, place, high).astype(BF16)
        push(near_out.at[index, 0], near_in.at[index, 0], near_sem.at[index, 0], to_up)
        wait_pair(down, place)
        near_out[index, 1] = paired(down, place, low).astype(BF16)
        push(near_out.at[index, 1], near_in.at[index, 1], near_sem.at[index, 1], to_down)
        arrived(far_in.at[index, 0], far_sem.at[index, 0])
        mixed_out[index, 0] = (paired(up, place, low) + far_in[index, 0].astype(F32)).astype(BF16)
        push(mixed_out.at[index, 0], mixed_in.at[index, 0], mixed_sem.at[index, 0], to_up)
        arrived(far_in.at[index, 1], far_sem.at[index, 1])
        mixed_out[index, 1] = (paired(down, place, high) + far_in[index, 1].astype(F32)).astype(BF16)
        push(mixed_out.at[index, 1], mixed_in.at[index, 1], mixed_sem.at[index, 1], to_down)
    local = lax.dot_general(
        grad_ref[...], w_self_ref[...], (((1,), (1,)), ((), ())), preferred_element_type=F32
    )

    def gathered(index):
        place = places[index]
        wait_pair(y, place)
        for part in range(2):
            arrived(near_in.at[index, part], near_sem.at[index, part])
        for part in range(2):
            arrived(mixed_in.at[index, part], mixed_sem.at[index, part])
        upper = paired(y, place, low) + mixed_in[index, 0].astype(F32) + near_in[index, 1].astype(F32)
        lower = paired(y, place, high) + near_in[index, 0].astype(F32) + mixed_in[index, 1].astype(F32)
        return jnp.concatenate([upper, lower], axis=0)

    for index in range(LINE - 1):
        line_out[index] = gathered(index).astype(BF16)
        push(line_out.at[index], line_in.at[index], line_sem.at[index], to_along[LINE - 2 - index])
    local += gathered(LINE - 1)
    for index in range(LINE - 1):
        arrived(line_in.at[index], line_sem.at[index])
        local += line_in[index].astype(F32)
    chosen = one_hot_order(order_ref, size).astype(F32).astype(BF16)
    moved = jnp.zeros_like(local)
    rest = local
    for _ in range(3):
        piece = rest.astype(BF16)
        moved += jnp.dot(chosen, piece, preferred_element_type=F32)
        rest -= piece.astype(F32)
    out_ref[...] = moved
    for copy in sent:
        copy.wait_send()


def scatter_rows(terms, grad_pre, w_self, order):
    size, channels = grad_pre.shape
    half = size // 2
    halves = functools.partial(pltpu.VMEM, dtype=BF16)
    return pl.pallas_call(
        scatter_kernel,
        out_shape=jax.ShapeDtypeStruct((size, channels), F32),
        in_specs=[pl.BlockSpec(memory_space=pltpu.VMEM)] * 4,
        out_specs=pl.BlockSpec(memory_space=pltpu.VMEM),
        scratch_shapes=[
            halves((LINE * LINE, size, channels)),
            halves((LINE, size, channels)),
            halves((LINE, 2, half, channels)),
            halves((LINE, 2, half, channels)),
            halves((LINE - 1, size, channels)),
            halves((LINE, 2, half, channels)),
            halves((LINE, 2, half, channels)),
            halves((LINE, 2, half, channels)),
            halves((LINE - 1, size, channels)),
            pltpu.SemaphoreType.DMA((43,)),
            pltpu.SemaphoreType.DMA((LINE * LINE,)),
            pltpu.SemaphoreType.DMA((LINE, 2)),
            pltpu.SemaphoreType.DMA((LINE, 2)),
            pltpu.SemaphoreType.DMA((LINE, 2)),
            pltpu.SemaphoreType.DMA((LINE - 1,)),
        ],
        compiler_params=pltpu.CompilerParams(collective_id=2, has_side_effects=True),
        name="scatter_rows",
    )(terms, grad_pre, w_self, order)


def shards(
    features,
    edge_tiles,
    tile_rows,
    tile_cols,
    tile_count,
    node_order,
    w_self,
    w_neigh,
    bias_term,
    cotangent,
):
    column = gather_rows(node_order, features)
    own = lax.dynamic_index_in_dim(column, lax.axis_index("row"), 0, keepdims=False)
    sums, degree = forward_sums(tile_count, tile_rows, tile_cols, edge_tiles, column)
    activations, grad_pre, self_part, neigh_part, bias_part, agg = middle(
        sums, degree, own, w_self, w_neigh, bias_term[None], cotangent
    )
    self_grad, neigh_grad, bias_grad = lax.psum((self_part, neigh_part, bias_part), ("row", "col"))
    terms = backward_terms(tile_count, tile_rows, tile_cols, edge_tiles, agg)
    feature_grad = scatter_rows(terms, grad_pre, w_self, node_order)
    return (activations, feature_grad, self_grad, neigh_grad, bias_grad[0])


def solution(mesh):
    placed = (
        P(("row", "col"), None),
        P(("row", "col"), None, None),
        P(("row", "col"), None),
        P(("row", "col"), None),
        P(("row", "col")),
        P(("row", "col"), None),
        P(),
        P(),
        P(),
        P(("row", "col"), None),
    )
    return jax.shard_map(
        shards,
        mesh=mesh,
        in_specs=placed,
        out_specs=(P(("row", "col"), None), P(("row", "col"), None), P(), P(), P()),
        check_vma=False,
    )
```

```python
import functools

import jax
import jax.numpy as jnp
from jax import lax
from jax.experimental import pallas as pl
from jax.experimental.pallas import tpu as pltpu
from jax.sharding import PartitionSpec as P

LINE = 4
CORES = 2
HALVES = 2
ROWS = LINE * LINE * CORES
COLS = LINE * HALVES
DEPTH = LINE * HALVES
LANES = 128
F32 = jnp.float32
BF16 = jnp.bfloat16


def row_place():
    me = lax.axis_index("row")
    return me // (LINE * CORES), (me // CORES) % LINE, me % CORES


def row_of(y, z, core):
    return (y * LINE + z) * CORES + core


def z_partners(z):
    return (z + 1 - 2 * (z % 2), (z + 2) % LINE, LINE - 1 - z)


def greet(targets):
    barrier = pltpu.get_barrier_semaphore()
    for target in targets:
        pl.semaphore_signal(barrier, inc=1, device_id=target, device_id_type=pl.DeviceIdType.MESH)
    pl.semaphore_wait(barrier, len(targets))


def start_copy(source, target, send_sem, recv_sem, device):
    copy = pltpu.make_async_remote_copy(
        src_ref=source,
        dst_ref=target,
        send_sem=send_sem,
        recv_sem=recv_sem,
        device_id=device,
        device_id_type=pl.DeviceIdType.MESH,
    )
    copy.start()
    return copy


def arrived(target, recv_sem):
    pltpu.make_async_copy(target, target, recv_sem).wait()


def one_hot_order(order_ref, size):
    return order_ref[...] == lax.broadcasted_iota(jnp.int32, (size, size), 0)


def gather_kernel(order_ref, feat_ref, column_ref, own_ref, send_sem, recv_sem, half_sem):
    y, z, core = row_place()
    size = feat_ref.shape[0]
    half = size // 2
    up, down, far = (y + 1) % LINE, (y + LINE - 1) % LINE, (y + 2) % LINE
    along = z_partners(z)
    other = {"row": row_of(y, z, 1 - core)}
    to_up = {"row": row_of(up, z, core)}
    to_down = {"row": row_of(down, z, core)}
    to_along = [{"row": row_of(y, place, core)} for place in along]
    me = row_of(y, z, core)
    chosen = one_hot_order(order_ref, size).astype(F32).astype(BF16)
    own = lax.dot_general(
        chosen, feat_ref[...], (((0,), (0,)), ((), ())), preferred_element_type=F32
    ).astype(BF16)
    own_ref[...] = own
    column_ref[me] = own
    greet([other, to_up, to_down, *to_along])
    sent = []

    def push(block, device):
        sent.append(
            start_copy(
                column_ref.at[block], column_ref.at[block], send_sem.at[len(sent)], recv_sem.at[block], device
            )
        )

    def push_half(block, slot, part, device):
        rows = pl.ds(part * half, half)
        sent.append(
            start_copy(
                column_ref.at[block, rows],
                column_ref.at[block, rows],
                send_sem.at[len(sent)],
                half_sem.at[slot, part],
                device,
            )
        )

    def wait_block(block):
        arrived(column_ref.at[block], recv_sem.at[block])

    def from_line(index):
        block = row_of(y, along[index], core)
        wait_block(block)
        push(block, to_up)
        push(block, to_down)
        push(block, other)

    places = (z, *along)

    def from_ring(index):
        below, above = row_of(down, places[index], core), row_of(up, places[index], core)
        wait_block(below)
        push_half(below, index, 0, to_up)
        push(below, other)
        wait_block(above)
        push_half(above, index, 1, to_down)
        push(above, other)

    def from_far(index):
        block = row_of(far, places[index], core)
        for part in range(2):
            arrived(column_ref.at[block, pl.ds(part * half, half)], half_sem.at[index, part])
        push(block, other)

    push(me, to_up)
    push(me, to_down)
    for device in to_along:
        push(me, device)
    push(me, other)
    from_line(0)
    from_ring(0)
    from_line(1)
    from_ring(1)
    from_line(2)
    from_far(0)
    from_ring(2)
    from_far(1)
    from_ring(3)
    from_far(2)
    from_far(3)
    for place in range(LINE * LINE):
        wait_block(place * CORES + 1 - core)
    for copy in sent:
        copy.wait_send()


def gather_rows(order, features):
    size, channels = features.shape
    return pl.pallas_call(
        gather_kernel,
        out_shape=(
            jax.ShapeDtypeStruct((ROWS, size, channels), BF16),
            jax.ShapeDtypeStruct((size, channels), BF16),
        ),
        in_specs=[pl.BlockSpec(memory_space=pltpu.VMEM)] * 2,
        out_specs=(pl.BlockSpec(memory_space=pltpu.VMEM),) * 2,
        scratch_shapes=[
            pltpu.SemaphoreType.DMA((35,)),
            pltpu.SemaphoreType.DMA((ROWS,)),
            pltpu.SemaphoreType.DMA((LINE, 2)),
        ],
        compiler_params=pltpu.CompilerParams(collective_id=0, has_side_effects=True),
        name="gather_rows",
    )(order, features)


def forward_kernel(count_ref, rows_ref, cols_ref, tiles_ref, column_ref, sums_ref, degree_ref):
    size = tiles_ref.shape[1]
    sums_ref[...] = jnp.zeros_like(sums_ref)
    degree_ref[...] = jnp.zeros_like(degree_ref)
    ones = jnp.ones((8, size), BF16)

    def advance(slot, carry):
        at = rows_ref[0, slot]
        tile = tiles_ref[slot]
        sums_ref[at] += jnp.dot(tile, column_ref[cols_ref[0, slot]], preferred_element_type=F32)
        degree_ref[at] += lax.dot_general(
            ones, tile, (((1,), (1,)), ((), ())), preferred_element_type=F32
        )
        return carry

    lax.fori_loop(0, count_ref[0], advance, 0)


def forward_sums(count, rows_at, cols_at, tiles, column):
    _, size, channels = column.shape
    return pl.pallas_call(
        forward_kernel,
        out_shape=(
            jax.ShapeDtypeStruct((COLS, size, channels), F32),
            jax.ShapeDtypeStruct((COLS, 8, size), F32),
        ),
        in_specs=[pl.BlockSpec(memory_space=pltpu.SMEM)] * 3 + [pl.BlockSpec(memory_space=pltpu.VMEM)] * 2,
        out_specs=(pl.BlockSpec(memory_space=pltpu.VMEM),) * 2,
        name="forward_sums",
    )(count, rows_at, cols_at, tiles, column)


def middle_kernel(
    sums_ref,
    degree_ref,
    own_ref,
    w_self_ref,
    w_neigh_ref,
    bias_ref,
    cot_ref,
    preact_ref,
    grad_ref,
    quarter_ref,
    bias_grad_ref,
    agg_ref,
    far_out,
    near_out,
    mixed_out,
    cross_out,
    far_in,
    near_in,
    mixed_in,
    cross_in,
    degree_in,
    pair_out,
    pair_in,
    weight_sum,
    weight_far,
    weight_near,
    weight_mixed,
    weight_mixed_out,
    bias_out,
    bias_in,
    send_sem,
    far_sem,
    near_sem,
    mixed_sem,
    cross_sem,
    degree_sem,
    agg_sem,
    agg_half_sem,
    pair_sem,
    weight_sem,
    bias_sem,
):
    here = lax.axis_index("col")
    x, side = here // HALVES, here % HALVES
    size, channels = own_ref.shape
    lanes = bias_grad_ref.shape[1]
    quarter = quarter_ref.shape[0]
    half = size // 2
    low, high = pl.ds(0, half), pl.ds(half, half)
    up, down, far = (x + 1) % LINE, (x + LINE - 1) % LINE, (x + 2) % LINE
    sides = (1 - side, side)

    def col_of(place, where):
        return place * HALVES + where

    to_up = {"col": col_of(up, side)}
    to_down = {"col": col_of(down, side)}
    to_cross = {"col": col_of(x, 1 - side)}
    peers = [to_up, to_down, to_cross, {"col": col_of(far, side)}]
    peers += [{"col": col_of(place, 1 - side)} for place in (up, down, far)]
    y, z, core = row_place()
    pair = {"row": row_of(y, z, 1 - core)}
    y_up, y_down, y_far = (y + 1) % LINE, (y + LINE - 1) % LINE, (y + 2) % LINE
    y_peers = [{"row": row_of(place, z, core)} for place in (y_up, y_down, y_far)]
    peers += [pair, *y_peers]
    sent = []

    def push(source, target, recv_sem, device):
        sent.append(start_copy(source, target, send_sem.at[len(sent)], recv_sem, device))

    greet(peers)
    for offset in range(1, COLS):
        owner = (here + offset) % COLS
        push(degree_ref.at[owner], degree_in.at[offset], degree_sem.at[offset], {"col": owner})
    for phase in range(2):
        block = col_of(far, sides[phase])
        far_out[phase] = sums_ref[block].astype(BF16)
        push(far_out.at[phase, low], far_in.at[phase, 0], far_sem.at[phase, 0], to_up)
        push(far_out.at[phase, high], far_in.at[phase, 1], far_sem.at[phase, 1], to_down)
        near_out[phase, 0] = sums_ref[col_of(up, sides[phase]), high].astype(BF16)
        near_out[phase, 1] = sums_ref[col_of(down, sides[phase]), low].astype(BF16)
        push(near_out.at[phase, 0], near_in.at[phase, 0], near_sem.at[phase, 0], to_up)
        push(near_out.at[phase, 1], near_in.at[phase, 1], near_sem.at[phase, 1], to_down)
    own = own_ref[...]
    self_term = jnp.dot(own, w_self_ref[...], preferred_element_type=F32) + bias_ref[...].astype(F32)

    def gathered(phase):
        arrived(far_in.at[phase, 0], far_sem.at[phase, 0])
        mixed_out[phase, 0] = (
            sums_ref[col_of(up, sides[phase]), low] + far_in[phase, 0].astype(F32)
        ).astype(BF16)
        push(mixed_out.at[phase, 0], mixed_in.at[phase, 0], mixed_sem.at[phase, 0], to_up)
        arrived(far_in.at[phase, 1], far_sem.at[phase, 1])
        mixed_out[phase, 1] = (
            sums_ref[col_of(down, sides[phase]), high] + far_in[phase, 1].astype(F32)
        ).astype(BF16)
        push(mixed_out.at[phase, 1], mixed_in.at[phase, 1], mixed_sem.at[phase, 1], to_down)
        for part in range(2):
            arrived(near_in.at[phase, part], near_sem.at[phase, part])
        for part in range(2):
            arrived(mixed_in.at[phase, part], mixed_sem.at[phase, part])
        mine = sums_ref[col_of(x, sides[phase])]
        upper = mine[:half] + mixed_in[phase, 0].astype(F32) + near_in[phase, 1].astype(F32)
        lower = mine[half:] + near_in[phase, 0].astype(F32) + mixed_in[phase, 1].astype(F32)
        return jnp.concatenate([upper, lower], axis=0)

    cross_out[...] = gathered(0).astype(BF16)
    push(cross_out, cross_in, cross_sem.at[0], to_cross)
    own_sum = gathered(1)
    degree = degree_ref[here]
    for offset in range(1, COLS):
        arrived(degree_in.at[offset], degree_sem.at[offset])
        degree += degree_in[offset]
    inverse = jnp.broadcast_to((1.0 / (1.0 + degree))[:1], (size, size)).T
    inverse = jnp.concatenate([inverse] * (own.shape[1] // size), axis=1)
    arrived(cross_in, cross_sem.at[0])
    own_sum += cross_in[...].astype(F32)
    neigh_mean = (own_sum * inverse).astype(BF16)
    preact = self_term + jnp.dot(neigh_mean, w_neigh_ref[...], preferred_element_type=F32)
    below = jnp.minimum(preact, 0.0)
    slope = cot_ref[...].astype(F32) * jnp.exp(below)
    grad_pre = slope.astype(BF16)
    agg_ref[here] = (
        lax.dot_general(grad_pre, w_neigh_ref[...], (((1,), (1,)), ((), ())), preferred_element_type=F32)
        * inverse
    ).astype(BF16)
    push(agg_ref.at[here], agg_ref.at[here], agg_sem.at[here], to_cross)
    push(agg_ref.at[here], agg_ref.at[here], agg_sem.at[here], to_up)
    push(agg_ref.at[here], agg_ref.at[here], agg_sem.at[here], to_down)
    grad_ref[...] = grad_pre
    preact_ref[...] = preact
    bias_part = jnp.sum(grad_pre.astype(F32), axis=0, keepdims=True)
    bias_out[0] = jnp.zeros_like(bias_out[0])
    for part in range(channels // lanes):
        bias_out[0, pl.ds(part, 1)] = bias_part[:, part * lanes : (part + 1) * lanes]
    push(bias_out.at[0], bias_in.at[0], bias_sem.at[0], pair)

    def weight_part(keep):
        left = jnp.where((core == 0) == keep, own, neigh_mean)
        return lax.dot_general(left, grad_pre, (((0,), (0,)), ((), ())), preferred_element_type=F32)

    pair_out[...] = weight_part(False)
    push(pair_out, pair_in, pair_sem.at[0], pair)
    weight_sum[...] = weight_part(True)

    def round_ring(where, slot):
        from_down, from_up = col_of(down, where), col_of(up, where)
        arrived(agg_ref.at[from_down], agg_sem.at[from_down])
        push(agg_ref.at[from_down, low], agg_ref.at[from_down, low], agg_half_sem.at[slot, 0], to_up)
        arrived(agg_ref.at[from_up], agg_sem.at[from_up])
        push(agg_ref.at[from_up, high], agg_ref.at[from_up, high], agg_half_sem.at[slot, 1], to_down)

    round_ring(side, 0)
    cross = col_of(x, 1 - side)
    arrived(agg_ref.at[cross], agg_sem.at[cross])
    push(agg_ref.at[cross], agg_ref.at[cross], agg_sem.at[cross], to_up)
    push(agg_ref.at[cross], agg_ref.at[cross], agg_sem.at[cross], to_down)

    def weight_rows(place, part):
        return pl.ds(pl.multiple_of(place * quarter + part * (quarter // 2), 8), quarter // 2)

    arrived(pair_in, pair_sem.at[0])
    weight_sum[...] += pair_in[...]
    for part in range(2):
        push(weight_sum.at[weight_rows(y_far, part)], weight_far.at[part], weight_sem.at[0, part], y_peers[part])
    near_rows = (weight_rows(y_up, 1), weight_rows(y_down, 0))
    for part in range(2):
        push(weight_sum.at[near_rows[part]], weight_near.at[part], weight_sem.at[1, part], y_peers[part])
    arrived(bias_in.at[0], bias_sem.at[0])
    bias_out[1] = bias_out[0] + bias_in[0]
    for offset, device in enumerate(y_peers):
        push(bias_out.at[1], bias_in.at[1 + offset], bias_sem.at[1 + offset], device)
    round_ring(1 - side, 1)
    mixed_rows = (weight_rows(y_up, 0), weight_rows(y_down, 1))
    for part in range(2):
        arrived(weight_far.at[part], weight_sem.at[0, part])
        weight_mixed_out[part] = weight_sum[mixed_rows[part]] + weight_far[part]
        push(weight_mixed_out.at[part], weight_mixed.at[part], weight_sem.at[2, part], y_peers[part])
    bias_total = bias_out[1]
    for offset in range(LINE - 1):
        arrived(bias_in.at[1 + offset], bias_sem.at[1 + offset])
        bias_total += bias_in[1 + offset]
    bias_grad_ref[...] = bias_total
    for slot, where in enumerate((side, 1 - side)):
        block = col_of(far, where)
        arrived(agg_ref.at[block, low], agg_half_sem.at[slot, 0])
        arrived(agg_ref.at[block, high], agg_half_sem.at[slot, 1])
    for part in range(2):
        arrived(weight_near.at[part], weight_sem.at[1, part])
        arrived(weight_mixed.at[part], weight_sem.at[2, part])
    for part in range(2):
        quarter_ref[pl.ds(part * (quarter // 2), quarter // 2)] = (
            weight_sum[weight_rows(y, part)] + weight_mixed[part] + weight_near[1 - part]
        )
    for copy in sent:
        copy.wait_send()


def middle(sums, degree, own, w_self, w_neigh, bias, cotangent):
    size, channels = own.shape
    half = size // 2
    wide = w_self.shape[0]
    eighth = wide // (2 * LINE)
    halves = functools.partial(pltpu.VMEM, dtype=BF16)
    return pl.pallas_call(
        middle_kernel,
        out_shape=(
            jax.ShapeDtypeStruct((size, channels), F32),
            jax.ShapeDtypeStruct((size, channels), BF16),
            jax.ShapeDtypeStruct((wide // LINE, wide), F32),
            jax.ShapeDtypeStruct((8, LANES), F32),
            jax.ShapeDtypeStruct((COLS, size, channels), BF16),
        ),
        in_specs=[pl.BlockSpec(memory_space=pltpu.VMEM)] * 7,
        out_specs=(pl.BlockSpec(memory_space=pltpu.VMEM),) * 5,
        scratch_shapes=[
            halves((2, size, channels)),
            halves((2, 2, half, channels)),
            halves((2, 2, half, channels)),
            halves((size, channels)),
            halves((2, 2, half, channels)),
            halves((2, 2, half, channels)),
            halves((2, 2, half, channels)),
            halves((size, channels)),
            pltpu.VMEM((COLS, 8, size), F32),
            pltpu.VMEM((wide, wide), F32),
            pltpu.VMEM((wide, wide), F32),
            pltpu.VMEM((wide, wide), F32),
            pltpu.VMEM((2, eighth, wide), F32),
            pltpu.VMEM((2, eighth, wide), F32),
            pltpu.VMEM((2, eighth, wide), F32),
            pltpu.VMEM((2, eighth, wide), F32),
            pltpu.VMEM((2, 8, LANES), F32),
            pltpu.VMEM((LINE, 8, LANES), F32),
            pltpu.SemaphoreType.DMA((40,)),
            pltpu.SemaphoreType.DMA((2, 2)),
            pltpu.SemaphoreType.DMA((2, 2)),
            pltpu.SemaphoreType.DMA((2, 2)),
            pltpu.SemaphoreType.DMA((1,)),
            pltpu.SemaphoreType.DMA((COLS,)),
            pltpu.SemaphoreType.DMA((COLS,)),
            pltpu.SemaphoreType.DMA((2, 2)),
            pltpu.SemaphoreType.DMA((1,)),
            pltpu.SemaphoreType.DMA((3, 2)),
            pltpu.SemaphoreType.DMA((LINE,)),
        ],
        compiler_params=pltpu.CompilerParams(collective_id=1, has_side_effects=True),
        name="middle",
    )(sums, degree, own, w_self, w_neigh, bias, cotangent)


def backward_kernel(count_ref, rows_ref, cols_ref, tiles_ref, agg_ref, preact_ref, terms_ref, act_ref, total):
    total[...] = jnp.zeros_like(total)

    def advance(slot, carry):
        at = cols_ref[0, slot]
        total[at] += lax.dot_general(
            tiles_ref[slot],
            agg_ref[rows_ref[0, slot]],
            (((0,), (0,)), ((), ())),
            preferred_element_type=F32,
        )
        return carry

    lax.fori_loop(0, count_ref[0], advance, 0)

    def put(block, carry):
        terms_ref[block % CORES, block // CORES] = total[block].astype(BF16)
        return carry

    lax.fori_loop(0, ROWS, put, 0)
    preact = preact_ref[...]
    bent = jnp.tanh(0.5 * jnp.minimum(preact, 0.0))
    act_ref[...] = (jnp.maximum(preact, 0.0) + 2.0 * bent / (1.0 - bent)).astype(BF16)


def backward_terms(count, rows_at, cols_at, tiles, agg, preact):
    _, size, channels = agg.shape
    return pl.pallas_call(
        backward_kernel,
        out_shape=(
            jax.ShapeDtypeStruct((CORES, ROWS // CORES, size, channels), BF16),
            jax.ShapeDtypeStruct((size, channels), BF16),
        ),
        in_specs=[pl.BlockSpec(memory_space=pltpu.SMEM)] * 3 + [pl.BlockSpec(memory_space=pltpu.VMEM)] * 3,
        out_specs=(pl.BlockSpec(memory_space=pltpu.VMEM),) * 2,
        scratch_shapes=[pltpu.VMEM((ROWS, size, channels), F32)],
        name="backward_terms",
    )(count, rows_at, cols_at, tiles, agg, preact)


def scatter_kernel(
    terms_ref,
    grad_ref,
    w_self_ref,
    quarter_ref,
    bias_ref,
    out_ref,
    weights_ref,
    bias_grad_ref,
    pair_in,
    far_out,
    near_out,
    mixed_out,
    line_out,
    far_in,
    near_in,
    mixed_in,
    line_in,
    x_in,
    z_out,
    z_in,
    bias_out,
    bias_in,
    send_sem,
    pair_sem,
    far_sem,
    near_sem,
    mixed_sem,
    line_sem,
    x_sem,
    z_sem,
    bias_sem,
    deep_sem,
    ring_sem,
    wide_sem,
    wide_half_sem,
    both_sem,
):
    y, z, core = row_place()
    size = grad_ref.shape[0]
    half = size // 2
    low, high = pl.ds(0, half), pl.ds(half, half)
    up, down, far = (y + 1) % LINE, (y + LINE - 1) % LINE, (y + 2) % LINE
    along = z_partners(z)
    places = (along[2], along[1], along[0], z)
    other = {"row": row_of(y, z, 1 - core)}
    to_up = {"row": row_of(up, z, core)}
    to_down = {"row": row_of(down, z, core)}
    to_along = [{"row": row_of(y, place, core)} for place in along]
    sent = []

    def push(source, target, recv_sem, device):
        sent.append(start_copy(source, target, send_sem.at[len(sent)], recv_sem, device))

    here = lax.axis_index("col")
    x, side = here // HALVES, here % HALVES
    deep = side * LINE + z
    x_up, x_down, x_far = (x + 1) % LINE, (x + LINE - 1) % LINE, (x + 2) % LINE

    def at_x(place):
        return {"col": place * HALVES + side}

    def at_deep(place):
        return {"row": row_of(y, place % LINE, core), "col": x * HALVES + place // LINE}

    y_peers = [to_up, to_down, {"row": row_of(far, z, core)}]
    deep_peers = [(deep + offset) % DEPTH for offset in range(1, DEPTH)]
    greet([other, *y_peers, *(at_deep(place) for place in deep_peers), at_x(x_up), at_x(x_down), at_x(x_far)])

    strip = x_in.shape[1]
    for offset in range(1, LINE):
        place = (x + offset) % LINE
        rows = pl.ds(pl.multiple_of(place * strip, 8), strip)
        push(quarter_ref.at[rows], x_in.at[offset], x_sem.at[offset], at_x(place))
        push(bias_ref, bias_in.at[offset], bias_sem.at[offset], at_x(place))

    def reduced_x():
        mine = quarter_ref[pl.ds(pl.multiple_of(x * strip, 8), strip)]
        bias = bias_ref[...]
        for offset in range(1, LINE):
            arrived(x_in.at[offset], x_sem.at[offset])
            mine += x_in[offset]
            arrived(bias_in.at[offset], bias_sem.at[offset])
            bias += bias_in[offset]
        low_rows = strip // 2
        for place in range(DEPTH):
            rows = slice((place % 2) * low_rows, (place % 2 + 1) * low_rows)
            z_out[place] = mine[rows, (place // 2) * LANES : (place // 2 + 1) * LANES]
        bias_out[...] = bias
        for offset, place in enumerate(deep_peers, 1):
            push(z_out.at[place], z_in.at[offset], z_sem.at[offset], at_deep(place))
            push(bias_out, bias_in.at[LINE + offset], bias_sem.at[LINE + offset], at_deep(place))

    def reduced_z():
        mine = z_out[deep]
        bias = bias_out[...]
        for offset in range(1, DEPTH):
            arrived(z_in.at[offset], z_sem.at[offset])
            mine += z_in[offset]
            arrived(bias_in.at[LINE + offset], bias_sem.at[LINE + offset])
            bias += bias_in[LINE + offset]
        bias_grad_ref[...] = bias
        piece = weights_ref.at[core, x, y, deep]
        weights_ref[core, x, y, deep] = mine
        for place in deep_peers:
            push(piece, piece, deep_sem.at[deep], at_deep(place))

    def gathered_z():
        for place in deep_peers:
            arrived(weights_ref.at[core, x, y, place], deep_sem.at[place])
        piece = weights_ref.at[core, x, y]
        for device in y_peers:
            push(piece, piece, ring_sem.at[y], device)

    def both_cores(place):
        piece = weights_ref.at[core, place]
        push(piece, piece, both_sem.at[place], other)

    def gathered_y():
        for place in (up, down, far):
            arrived(weights_ref.at[core, x, place], ring_sem.at[place])
        piece = weights_ref.at[core, x]
        push(piece, piece, wide_sem.at[x], at_x(x_up))
        push(piece, piece, wide_sem.at[x], at_x(x_down))
        both_cores(x)

    def gathered_near_x():
        for part, (source, target) in enumerate(((x_down, x_up), (x_up, x_down))):
            arrived(weights_ref.at[core, source], wide_sem.at[source])
            piece = weights_ref.at[core, source, pl.ds(part * (LINE // 2), LINE // 2)]
            push(piece, piece, wide_half_sem.at[part], at_x(target))
            both_cores(source)

    def gathered_x():
        for part in range(2):
            piece = weights_ref.at[core, x_far, pl.ds(part * (LINE // 2), LINE // 2)]
            arrived(piece, wide_half_sem.at[part])
        both_cores(x_far)
        for place in range(LINE):
            arrived(weights_ref.at[1 - core, place], both_sem.at[place])

    for ring in (far, up, down, y):
        for place in places:
            block = ring * LINE + place
            push(terms_ref.at[1 - core, block], pair_in.at[block], pair_sem.at[block], other)

    def paired(ring, place, rows):
        block = ring * LINE + place
        return terms_ref[core, block, rows].astype(F32) + pair_in[block, rows].astype(F32)

    def wait_pair(ring, place):
        block = ring * LINE + place
        arrived(pair_in.at[block], pair_sem.at[block])

    everything = pl.ds(0, size)
    for index, place in enumerate(places):
        wait_pair(far, place)
        far_out[index] = paired(far, place, everything).astype(BF16)
        push(far_out.at[index, low], far_in.at[index, 0], far_sem.at[index, 0], to_up)
        push(far_out.at[index, high], far_in.at[index, 1], far_sem.at[index, 1], to_down)
    reduced_x()
    for index, place in enumerate(places):
        if index == 2:
            reduced_z()
        if index == LINE - 1:
            gathered_z()
        wait_pair(up, place)
        near_out[index, 0] = paired(up, place, high).astype(BF16)
        push(near_out.at[index, 0], near_in.at[index, 0], near_sem.at[index, 0], to_up)
        wait_pair(down, place)
        near_out[index, 1] = paired(down, place, low).astype(BF16)
        push(near_out.at[index, 1], near_in.at[index, 1], near_sem.at[index, 1], to_down)
        arrived(far_in.at[index, 0], far_sem.at[index, 0])
        mixed_out[index, 0] = (paired(up, place, low) + far_in[index, 0].astype(F32)).astype(BF16)
        push(mixed_out.at[index, 0], mixed_in.at[index, 0], mixed_sem.at[index, 0], to_up)
        arrived(far_in.at[index, 1], far_sem.at[index, 1])
        mixed_out[index, 1] = (paired(down, place, high) + far_in[index, 1].astype(F32)).astype(BF16)
        push(mixed_out.at[index, 1], mixed_in.at[index, 1], mixed_sem.at[index, 1], to_down)
    local = lax.dot_general(
        grad_ref[...], w_self_ref[...], (((1,), (1,)), ((), ())), preferred_element_type=F32
    )

    def gathered(index):
        place = places[index]
        wait_pair(y, place)
        for part in range(2):
            arrived(near_in.at[index, part], near_sem.at[index, part])
        for part in range(2):
            arrived(mixed_in.at[index, part], mixed_sem.at[index, part])
        upper = paired(y, place, low) + mixed_in[index, 0].astype(F32) + near_in[index, 1].astype(F32)
        lower = paired(y, place, high) + near_in[index, 0].astype(F32) + mixed_in[index, 1].astype(F32)
        return jnp.concatenate([upper, lower], axis=0)

    for index in range(LINE - 1):
        line_out[index] = gathered(index).astype(BF16)
        push(line_out.at[index], line_in.at[index], line_sem.at[index], to_along[LINE - 2 - index])
        if index == 1:
            gathered_y()
    local += gathered(LINE - 1)
    gathered_near_x()
    for index in range(LINE - 1):
        arrived(line_in.at[index], line_sem.at[index])
        local += line_in[index].astype(F32)
    out_ref[...] = local
    gathered_x()
    for copy in sent:
        copy.wait_send()


def scatter_rows(terms, grad_pre, w_self, quarter, bias):
    size, channels = grad_pre.shape
    half = size // 2
    strip = quarter.shape[0] // LINE
    piece = (strip // 2, LANES)
    halves = functools.partial(pltpu.VMEM, dtype=BF16)
    return pl.pallas_call(
        scatter_kernel,
        out_shape=(
            jax.ShapeDtypeStruct((size, channels), F32),
            jax.ShapeDtypeStruct((CORES, LINE, LINE, DEPTH, *piece), F32),
            jax.ShapeDtypeStruct(bias.shape, F32),
        ),
        in_specs=[pl.BlockSpec(memory_space=pltpu.VMEM)] * 5,
        out_specs=(pl.BlockSpec(memory_space=pltpu.VMEM),) * 3,
        scratch_shapes=[
            halves((LINE * LINE, size, channels)),
            halves((LINE, size, channels)),
            halves((LINE, 2, half, channels)),
            halves((LINE, 2, half, channels)),
            halves((LINE - 1, size, channels)),
            halves((LINE, 2, half, channels)),
            halves((LINE, 2, half, channels)),
            halves((LINE, 2, half, channels)),
            halves((LINE - 1, size, channels)),
            pltpu.VMEM((LINE, strip, quarter.shape[1]), F32),
            pltpu.VMEM((DEPTH, *piece), F32),
            pltpu.VMEM((DEPTH, *piece), F32),
            pltpu.VMEM(bias.shape, F32),
            pltpu.VMEM((LINE + DEPTH, *bias.shape), F32),
            pltpu.SemaphoreType.DMA((90,)),
            pltpu.SemaphoreType.DMA((LINE * LINE,)),
            pltpu.SemaphoreType.DMA((LINE, 2)),
            pltpu.SemaphoreType.DMA((LINE, 2)),
            pltpu.SemaphoreType.DMA((LINE, 2)),
            pltpu.SemaphoreType.DMA((LINE - 1,)),
            pltpu.SemaphoreType.DMA((LINE,)),
            pltpu.SemaphoreType.DMA((DEPTH,)),
            pltpu.SemaphoreType.DMA((LINE + DEPTH,)),
            pltpu.SemaphoreType.DMA((DEPTH,)),
            pltpu.SemaphoreType.DMA((LINE,)),
            pltpu.SemaphoreType.DMA((LINE,)),
            pltpu.SemaphoreType.DMA((2,)),
            pltpu.SemaphoreType.DMA((LINE,)),
        ],
        compiler_params=pltpu.CompilerParams(collective_id=2, has_side_effects=True),
        name="scatter_rows",
    )(terms, grad_pre, w_self, quarter, bias)


def finish_kernel(order_ref, local_ref, weights_ref, bias_ref, feature_ref, self_ref, neigh_ref, bias_grad_ref):
    size = local_ref.shape[0]
    chosen = one_hot_order(order_ref, size).astype(F32).astype(BF16)
    rest = local_ref[...]
    moved = jnp.zeros_like(rest)
    for _ in range(3):
        piece = rest.astype(BF16)
        moved += jnp.dot(chosen, piece, preferred_element_type=F32)
        rest -= piece.astype(F32)
    feature_ref[...] = moved
    low_rows = weights_ref.shape[4]

    def put(index, carry):
        x, y = index // LINE, index % LINE
        for core, target in enumerate((self_ref, neigh_ref)):
            for place in range(DEPTH):
                row = pl.multiple_of((y * LINE + x) * 2 * low_rows + (place % 2) * low_rows, 8)
                target[pl.ds(row, low_rows), pl.ds((place // 2) * LANES, LANES)] = weights_ref[core, x, y, place]
        return carry

    lax.fori_loop(0, LINE * LINE, put, 0)
    for part in range(bias_grad_ref.shape[1] // LANES):
        bias_grad_ref[:, pl.ds(part * LANES, LANES)] = bias_ref[pl.ds(part, 1)]


def finish(order, local, weights, bias):
    wide = local.shape[1]
    return pl.pallas_call(
        finish_kernel,
        out_shape=(
            jax.ShapeDtypeStruct(local.shape, F32),
            jax.ShapeDtypeStruct((wide, wide), F32),
            jax.ShapeDtypeStruct((wide, wide), F32),
            jax.ShapeDtypeStruct((1, wide), F32),
        ),
        in_specs=[pl.BlockSpec(memory_space=pltpu.VMEM)] * 4,
        out_specs=(pl.BlockSpec(memory_space=pltpu.VMEM),) * 4,
        name="finish",
    )(order, local, weights, bias)


def shards(
    features,
    edge_tiles,
    tile_rows,
    tile_cols,
    tile_count,
    node_order,
    w_self,
    w_neigh,
    bias_term,
    cotangent,
):
    column, own = gather_rows(node_order, features)
    sums, degree = forward_sums(tile_count, tile_rows, tile_cols, edge_tiles, column)
    preact, grad_pre, quarter, bias_part, agg = middle(
        sums, degree, own, w_self, w_neigh, bias_term[None], cotangent
    )
    terms, activations = backward_terms(tile_count, tile_rows, tile_cols, edge_tiles, agg, preact)
    local, weights, bias_sum = scatter_rows(terms, grad_pre, w_self, quarter, bias_part)
    feature_grad, self_grad, neigh_grad, bias_grad = finish(node_order, local, weights, bias_sum)
    return (activations, feature_grad, self_grad, neigh_grad, bias_grad[0])


def solution(mesh):
    placed = (
        P(("row", "col"), None),
        P(("row", "col"), None, None),
        P(("row", "col"), None),
        P(("row", "col"), None),
        P(("row", "col")),
        P(("row", "col"), None),
        P(),
        P(),
        P(),
        P(("row", "col"), None),
    )
    return jax.shard_map(
        shards,
        mesh=mesh,
        in_specs=placed,
        out_specs=(P(("row", "col"), None), P(("row", "col"), None), P(), P(), P()),
        check_vma=False,
    )
```
